32 devices in a mesh: req: 16 (over z, y, x), mlp: 2 (over core).
Axes of the slice: x: 2, y: 2, z: 4, core: 2. Of those that a mesh axis runs over, the one named last changes fastest.
Arguments:
- queries: bfloat16 [16, 256, 1536], P('req'), may hold values from -90 to 90
- cached_key_slots: bfloat16 [16, 8192, 512], P('req', 'mlp'), may hold values from -5 to 5
- cached_value_slots: bfloat16 [16, 8192, 512], P('req', 'mlp'), may hold values from -6 to 6
- new_token_keys: bfloat16 [16, 256, 512], P('req', 'mlp'), may hold values from -5.05 to 5.05
- new_token_values: bfloat16 [16, 256, 512], P('req', 'mlp'), may hold values from -6 to 6
- cache_len: int32 [16], replicated, may hold values from 1 to 8192, 65536 in all
- placing: int32 [16], replicated, may hold values from 0 to 15, each once
- w_gate: bfloat16 [1536, 12288], P('req', 'mlp'), may hold values from -0.15625 to 0.15625
- w_up: bfloat16 [1536, 12288], P('req', 'mlp'), may hold values from -0.15625 to 0.15625
- w_down: bfloat16 [12288, 1536], P('mlp', 'req'), may hold values from -0.0546875 to 0.0546875
Outputs:
- mixed: bfloat16 [16, 256, 1536], P('req', 'mlp')
The draws below stay inside these ranges and needn't reach their ends.
All inputs are finite; a program needn't handle non-finite values.
Results may differ from the reference program's by a relative error of at most 0.019.
Values may be sent and summed in bfloat16 or wider, within the bound.
A program may use at most 192 MiB of HBM per device.

```python
import math
import jax
import jax.numpy as jnp
import numpy as np
from jax import lax

HEAD_SIZE = 256
QUERY_HEADS = 6
KEY_VALUE_HEADS = 2
D = 1536
FF = 12288
NEW_TOKENS = 256
CACHE_SLOTS = 8192
REQUEST_COUNT = 16


def leading_keys(key):
    return jnp.clip(jax.random.normal(jax.random.fold_in(key, 11), (REQUEST_COUNT, KEY_VALUE_HEADS * HEAD_SIZE), jnp.float32), -5.0, 5.0)


def draw_cached_key_slots(key, part):
    remaining_items = jnp.clip(jax.random.normal(jax.random.fold_in(key, 12), (REQUEST_COUNT, CACHE_SLOTS, KEY_VALUE_HEADS * HEAD_SIZE), jnp.float32), -5.0, 5.0)
    position = jnp.arange(CACHE_SLOTS)[None, :, None]
    remaining_items = jnp.where(position == 0, leading_keys(key)[:, None, :], remaining_items)
    return remaining_items.astype(jnp.bfloat16)


def draw_queries(key, part):
    start_offset = jnp.clip(jax.random.normal(jax.random.fold_in(key, 13), (REQUEST_COUNT, NEW_TOKENS, QUERY_HEADS * HEAD_SIZE), jnp.float32), -5.0, 5.0)
    return start_offset.astype(jnp.bfloat16)


def draw_new_token_keys(key, part):
    start_offset = jnp.clip(jax.random.normal(jax.random.fold_in(key, 14), (REQUEST_COUNT, NEW_TOKENS, KEY_VALUE_HEADS * HEAD_SIZE), jnp.float32), -5.0, 5.0)
    return start_offset.astype(jnp.bfloat16)


def steps_of(rng, dims, shards, least, high):
    loudness, own = 1.0, jax.random.fold_in(rng, 6)
    for dim, shards_of in shards:
        steps = jnp.exp(jax.random.uniform(jax.random.fold_in(own, dim), (shards_of,), jnp.float32, least / len(shards), high / len(shards)))
        loudness = loudness * jnp.repeat(steps, dims[dim] // shards_of).reshape([-1 if axis == dim else 1 for axis in range(len(dims))])
    return loudness


def profile(amount, total, limit, skew):
    portions = [(1 << 20) // math.isqrt(standing ** skew) + 1 for standing in range(2, amount + 1)]
    spare, given = total - limit - (amount - 1), [1] * (amount - 1)
    while spare > 0:
        candidates = [i for i in range(amount - 1) if given[i] < limit]
        mass, left = sum([portions[i] for i in candidates]), spare
        for i in candidates:
            extra = min(limit - given[i], max(1, left * portions[i] // mass), spare)
            given[i] = given[i] + extra
            spare = spare - extra
    return np.array([limit] + given)


def uneven(own_key, count, total, limit, skew):
    if count == 2:
        one = jax.random.randint(own_key, (), max(1, total - limit), min(limit, total - 1) + 1)
        return jnp.stack([one, total - one])
    sizes = jnp.asarray(profile(count, total, limit, skew), jnp.int32)
    twos = (count - 1) // 2
    source_of, sink = sizes[1:1 + 2 * twos:2], sizes[2:2 + 2 * twos:2]
    room = jnp.minimum(source_of - 1, limit - sink)
    passed = jax.random.randint(jax.random.fold_in(own_key, 1), (twos,), 0, 1 << 20) % (room + 1)
    sizes = sizes.at[1:1 + 2 * twos:2].set(source_of - passed).at[2:2 + 2 * twos:2].set(sink + passed)
    return sizes[jax.random.permutation(jax.random.fold_in(own_key, 2), count)]


def scatter_about(rng, shape, scale, most, cuts=(), kind=jnp.bfloat16):
    values = scale * jax.random.normal(rng, shape, jnp.float32)
    if cuts:
        values = values * steps_of(rng, shape, cuts, -0.22, 0.18)
    return jnp.clip(values, -most, most).astype(kind)


def setup_inputs(seed: int = 0) -> dict:
    key_of = jax.random.split(jax.random.key(seed), 11)
    queries = draw_queries(jax.random.fold_in(key_of[10], 71), 0)
    cached_key_slots = draw_cached_key_slots(jax.random.fold_in(key_of[10], 71), 0)
    cached_value_slots = scatter_about(key_of[2], (REQUEST_COUNT, CACHE_SLOTS, KEY_VALUE_HEADS * HEAD_SIZE), 1.0, 6.0, ((0, 16), (1, 2)))
    new_token_keys = draw_new_token_keys(jax.random.fold_in(key_of[10], 71), 0)
    new_token_values = scatter_about(key_of[4], (REQUEST_COUNT, NEW_TOKENS, KEY_VALUE_HEADS * HEAD_SIZE), 1.0, 6.0, ((0, 16), (1, 2)))
    cache_len = uneven(key_of[5], REQUEST_COUNT, REQUEST_COUNT * CACHE_SLOTS // 2, CACHE_SLOTS, 2).astype(jnp.int32)
    placing = jax.random.permutation(key_of[6], REQUEST_COUNT).astype(jnp.int32)
    w_gate = scatter_about(key_of[7], (D, FF), D ** -0.5, 0.15625, ((0, 16), (1, 2)))
    w_up = scatter_about(key_of[8], (D, FF), D ** -0.5, 0.15625, ((0, 16), (1, 2)))
    w_down = scatter_about(key_of[9], (FF, D), FF ** -0.5, 0.0546875, ((0, 2), (1, 16)))
    return dict(queries=queries, cached_key_slots=cached_key_slots, cached_value_slots=cached_value_slots, new_token_keys=new_token_keys, new_token_values=new_token_values, cache_len=cache_len, placing=placing, w_gate=w_gate, w_up=w_up, w_down=w_down)


score_scale = 0.0625
negative = -1e+30

def attend_slot(query_token_rows, joined_keys, joined_values, new_key_rows, new_value_rows, live_len):
    query_group_width = QUERY_HEADS // KEY_VALUE_HEADS
    query_head_rows = query_token_rows.astype(jnp.float32).reshape(NEW_TOKENS, KEY_VALUE_HEADS, query_group_width, HEAD_SIZE)
    key_head_rows = joined_keys.astype(jnp.float32).reshape(CACHE_SLOTS, KEY_VALUE_HEADS, HEAD_SIZE)
    value_head_rows = joined_values.astype(jnp.float32).reshape(CACHE_SLOTS, KEY_VALUE_HEADS, HEAD_SIZE)
    new_token_keys = new_key_rows.astype(jnp.float32).reshape(NEW_TOKENS, KEY_VALUE_HEADS, HEAD_SIZE)
    new_token_values = new_value_rows.astype(jnp.float32).reshape(NEW_TOKENS, KEY_VALUE_HEADS, HEAD_SIZE)
    scores_old = jnp.einsum('ngrd,cgd->grnc', query_head_rows, key_head_rows) * score_scale
    cache_live = jnp.arange(CACHE_SLOTS, dtype=jnp.int32) < live_len
    scores_old = jnp.where(cache_live[None, None, None, :], scores_old, negative)
    scores_new = jnp.einsum('ngrd,mgd->grnm', query_head_rows, new_token_keys) * score_scale
    causal = jnp.arange(NEW_TOKENS, dtype=jnp.int32)[None, :] <= jnp.arange(NEW_TOKENS, dtype=jnp.int32)[:, None]
    scores_new = jnp.where(causal[None, None], scores_new, negative)
    row_top = jnp.maximum(scores_old.max(-1), scores_new.max(-1))
    expo_old = jnp.exp(scores_old - row_top[..., None])
    expo_new = jnp.exp(scores_new - row_top[..., None])
    denom = expo_old.sum(-1) + expo_new.sum(-1)
    probs_old = lax.optimization_barrier(expo_old.astype(jnp.bfloat16)).astype(jnp.float32)
    probs_new = lax.optimization_barrier(expo_new.astype(jnp.bfloat16)).astype(jnp.float32)
    weighted = jnp.einsum('grnc,cgd->ngrd', probs_old, value_head_rows)
    weighted = weighted + jnp.einsum('grnm,mgd->ngrd', probs_new, new_token_values)
    attended = weighted / jnp.transpose(denom, (2, 0, 1))[..., None]
    return attended.reshape(NEW_TOKENS, QUERY_HEADS * HEAD_SIZE).astype(jnp.bfloat16)

def reference(queries, cached_key_slots, cached_value_slots, new_token_keys, new_token_values, cache_len, placing, w_gate, w_up, w_down):
    live = cache_len[placing].astype(jnp.int32)

    def one_slot(items):
        query_token_rows, joined_keys, joined_values, new_key_rows, new_value_rows, live_len = items
        attended = attend_slot(query_token_rows, joined_keys, joined_values, new_key_rows, new_value_rows, live_len)
        wide = attended.astype(jnp.float32)
        normed = (wide * lax.rsqrt(lax.optimization_barrier(jnp.mean(wide * wide, axis=-1, keepdims=True)) + 1e-06)).astype(jnp.bfloat16)
        gate = jnp.dot(normed, w_gate, preferred_element_type=jnp.float32)
        upper = jnp.dot(normed, w_up, preferred_element_type=jnp.float32)
        hidden = (jax.nn.silu(gate) * upper).astype(jnp.bfloat16)
        down = jnp.dot(hidden, w_down, preferred_element_type=jnp.float32)
        return (wide + down).astype(jnp.bfloat16)
    return lax.map(one_slot, (queries, cached_key_slots, cached_value_slots, new_token_keys, new_token_values, live))
```

```python
import jax
import jax.numpy as jnp
from jax import lax
from jax.sharding import PartitionSpec as P

HEAD_SIZE = 256
QUERY_HEADS = 6
KEY_VALUE_HEADS = 2


score_scale = 0.0625
negative = -1e30


def lookup(table, index):
    positions = jnp.arange(table.shape[0], dtype=jnp.int32)
    return jnp.sum(jnp.where(positions == index, table, 0))


def rms_rows(attended):
    wide = attended.astype(jnp.float32)
    return (wide * lax.rsqrt(jnp.mean(wide * wide, axis=-1, keepdims=True) + 1e-06)).astype(
        jnp.bfloat16
    )


def gathered_weights(weighted, denom_local, w_gate, w_up, w_down):
    token_inputs = weighted.shape[0]
    mlp_index = lax.axis_index("mlp")
    row_count = token_inputs // lax.axis_size("mlp")
    weighted, denom = lax.psum((weighted, denom_local), "mlp")
    attended = (
        (weighted / jnp.transpose(denom, (2, 0, 1))[..., None])
        .reshape(token_inputs, QUERY_HEADS * HEAD_SIZE)
        .astype(jnp.bfloat16)
    )
    normed = rms_rows(attended)
    own_attended = lax.dynamic_slice_in_dim(attended, mlp_index * row_count, row_count, 0)
    gate_sum = jnp.dot(
        normed,
        lax.all_gather(w_gate, "req", axis=0, tiled=True),
        preferred_element_type=jnp.float32,
    )
    upper_sum = jnp.dot(
        normed, lax.all_gather(w_up, "req", axis=0, tiled=True), preferred_element_type=jnp.float32
    )
    hidden = (jax.nn.silu(gate_sum) * upper_sum).astype(jnp.bfloat16)
    partial_down = jnp.dot(
        hidden,
        lax.all_gather(w_down, "req", axis=1, tiled=True),
        preferred_element_type=jnp.float32,
    )
    own_rows = lax.psum_scatter(
        partial_down.astype(jnp.bfloat16), "mlp", scatter_dimension=0, tiled=True
    ).astype(jnp.float32)
    residual = own_attended.astype(jnp.float32)
    return (residual + own_rows).astype(jnp.bfloat16)[None]


def body(
    queries,
    cached_key_slots,
    cached_value_slots,
    new_token_keys,
    new_token_values,
    cache_len,
    placing,
    w_gate,
    w_up,
    w_down,
):
    slot_index = lax.axis_index("req")
    mlp_index = lax.axis_index("mlp")
    mlp_count = lax.axis_size("mlp")
    token_inputs = queries.shape[1]
    request_cache = cached_key_slots.shape[1]
    request_new_tokens = new_token_keys.shape[1]
    query_group_width = QUERY_HEADS // KEY_VALUE_HEADS
    row_count = token_inputs // mlp_count
    request = lookup(placing, slot_index)
    live_len = lookup(cache_len, request)
    query_head_rows = queries[0].reshape(
        token_inputs, KEY_VALUE_HEADS, query_group_width, HEAD_SIZE
    )
    request_keys = cached_key_slots[0].reshape(request_cache, KEY_VALUE_HEADS, HEAD_SIZE)
    request_values = cached_value_slots[0].reshape(request_cache, KEY_VALUE_HEADS, HEAD_SIZE)
    new_key_rows = new_token_keys[0].reshape(request_new_tokens, KEY_VALUE_HEADS, HEAD_SIZE)
    new_value_rows = new_token_values[0].reshape(request_new_tokens, KEY_VALUE_HEADS, HEAD_SIZE)
    cache_pos = mlp_index * request_cache + jnp.arange(request_cache, dtype=jnp.int32)
    cache_live = cache_pos < live_len
    scores_old = (
        jnp.einsum(
            "ngrd,cgd->grnc", query_head_rows, request_keys, preferred_element_type=jnp.float32
        )
        * score_scale
    )
    scores_old = jnp.where(cache_live[None, None, None, :], scores_old, negative)
    fresh_pos = mlp_index * request_new_tokens + jnp.arange(request_new_tokens, dtype=jnp.int32)
    causal = fresh_pos[None, :] <= jnp.arange(token_inputs, dtype=jnp.int32)[:, None]
    scores_new = (
        jnp.einsum(
            "ngrd,mgd->grnm", query_head_rows, new_key_rows, preferred_element_type=jnp.float32
        )
        * score_scale
    )
    scores_new = jnp.where(causal[None, None], scores_new, negative)
    local_top = jnp.maximum(scores_old.max(-1), scores_new.max(-1))
    row_top = lax.pmax(local_top, "mlp")
    expo_old = jnp.exp(scores_old - row_top[..., None])
    expo_new = jnp.exp(scores_new - row_top[..., None])
    denom_local = expo_old.sum(-1) + expo_new.sum(-1)
    probs_old = expo_old.astype(jnp.bfloat16)
    probs_new = expo_new.astype(jnp.bfloat16)
    weighted = jnp.einsum(
        "grnc,cgd->ngrd", probs_old, request_values, preferred_element_type=jnp.float32
    )
    weighted = weighted + jnp.einsum(
        "grnm,mgd->ngrd", probs_new, new_value_rows, preferred_element_type=jnp.float32
    )
    if lax.axis_size("req") > 16:
        return gathered_weights(weighted, denom_local, w_gate, w_up, w_down)
    w_in = jnp.stack([w_gate, w_up])
    w_in = lax.all_to_all(w_in, "req", split_axis=2, concat_axis=1, tiled=True)
    w_in = lax.all_gather(w_in, "mlp", axis=2, tiled=True)
    w_out = lax.all_to_all(w_down, "req", split_axis=0, concat_axis=1, tiled=True)
    w_out = lax.all_gather(w_out, "mlp", axis=0, tiled=True)
    denom_rows = jnp.transpose(denom_local, (2, 0, 1))
    weighted = lax.psum_scatter(weighted, "mlp", scatter_dimension=0, tiled=True)
    denom = lax.psum_scatter(denom_rows, "mlp", scatter_dimension=0, tiled=True)
    attended = (
        (weighted / denom[..., None])
        .reshape(row_count, QUERY_HEADS * HEAD_SIZE)
        .astype(jnp.bfloat16)
    )
    normed = lax.all_gather(rms_rows(attended), "req", axis=0, tiled=True)
    gate_sum = jnp.dot(normed, w_in[0], preferred_element_type=jnp.float32)
    upper_sum = jnp.dot(normed, w_in[1], preferred_element_type=jnp.float32)
    hidden = (jax.nn.silu(gate_sum) * upper_sum).astype(jnp.bfloat16)
    partial_down = jnp.dot(hidden, w_out, preferred_element_type=jnp.float32)
    own_rows = lax.psum_scatter(
        partial_down.astype(jnp.bfloat16), "req", scatter_dimension=0, tiled=True
    ).astype(jnp.float32)
    return (attended.astype(jnp.float32) + own_rows).astype(jnp.bfloat16)[None]


def solution(mesh):
    in_specs = (
        P("req", None, None),
        P("req", "mlp", None),
        P("req", "mlp", None),
        P("req", "mlp", None),
        P("req", "mlp", None),
        P(),
        P(),
        P("req", "mlp"),
        P("req", "mlp"),
        P("mlp", "req"),
    )
    out_specs = P("req", "mlp", None)
    return jax.shard_map(body, mesh=mesh, in_specs=in_specs, out_specs=out_specs, check_vma=False)
```

```python
import jax
import jax.numpy as jnp
from jax import lax
from jax.experimental import pallas as pl
from jax.experimental.pallas import tpu as pltpu
from jax.sharding import PartitionSpec as P

HEAD_SIZE = 256
QUERY_HEADS = 6
KEY_VALUE_HEADS = 2


score_scale = 0.0625
negative = -1e30


def lookup(table, index):
    positions = jnp.arange(table.shape[0], dtype=jnp.int32)
    return jnp.sum(jnp.where(positions == index, table, 0))


def rms_rows(attended):
    wide = attended.astype(jnp.float32)
    return (wide * lax.rsqrt(jnp.mean(wide * wide, axis=-1, keepdims=True) + 1e-06)).astype(
        jnp.bfloat16
    )


def gathered_weights(weighted, denom_local, w_gate, w_up, w_down):
    token_inputs = weighted.shape[0]
    mlp_index = lax.axis_index("mlp")
    row_count = token_inputs // lax.axis_size("mlp")
    weighted, denom = lax.psum((weighted, denom_local), "mlp")
    attended = (
        (weighted / jnp.transpose(denom, (2, 0, 1))[..., None])
        .reshape(token_inputs, QUERY_HEADS * HEAD_SIZE)
        .astype(jnp.bfloat16)
    )
    normed = rms_rows(attended)
    own_attended = lax.dynamic_slice_in_dim(attended, mlp_index * row_count, row_count, 0)
    gate_sum = jnp.dot(
        normed,
        lax.all_gather(w_gate, "req", axis=0, tiled=True),
        preferred_element_type=jnp.float32,
    )
    upper_sum = jnp.dot(
        normed, lax.all_gather(w_up, "req", axis=0, tiled=True), preferred_element_type=jnp.float32
    )
    hidden = (jax.nn.silu(gate_sum) * upper_sum).astype(jnp.bfloat16)
    partial_down = jnp.dot(
        hidden,
        lax.all_gather(w_down, "req", axis=1, tiled=True),
        preferred_element_type=jnp.float32,
    )
    own_rows = lax.psum_scatter(
        partial_down.astype(jnp.bfloat16), "mlp", scatter_dimension=0, tiled=True
    ).astype(jnp.float32)
    residual = own_attended.astype(jnp.float32)
    return (residual + own_rows).astype(jnp.bfloat16)[None]


def neighbours():
    me = lax.axis_index("req")
    planes = lax.axis_size("req") // 4
    plane, place = me // 4, me % 4
    beside = plane * 4 + place + 1 - 2 * (place % 2)
    above = plane * 4 + (place + 2) % 4
    along = [((plane + k) % planes) * 4 + place for k in range(planes)]
    return me, beside, above, along


def greet(peers):
    barrier = pltpu.get_barrier_semaphore()
    for peer in peers:
        pl.semaphore_signal(
            barrier, inc=1, device_id={"req": peer}, device_id_type=pl.DeviceIdType.MESH
        )
    pl.semaphore_wait(barrier, len(peers))


def push(source, target, send_sem, recv_sem, peer):
    copy = pltpu.make_async_remote_copy(
        src_ref=source,
        dst_ref=target,
        send_sem=send_sem,
        recv_sem=recv_sem,
        device_id={"req": peer},
        device_id_type=pl.DeviceIdType.MESH,
    )
    copy.start()
    return copy


def gather_kernel(own_ref, out_ref, send_sem, recv_sem, own_sem):
    me, beside, above, along = neighbours()
    planes = len(along)
    greet([beside, above] + along[1:])
    sent = []

    def forward(block, peer, source=None):
        sent.append(
            push(
                out_ref.at[block] if source is None else source,
                out_ref.at[block],
                send_sem.at[len(sent)],
                recv_sem.at[block],
                peer,
            )
        )

    def arrived(block):
        pltpu.make_async_copy(out_ref.at[block], out_ref.at[block], recv_sem.at[block]).wait()

    for k in range(1, planes):
        forward(me, along[k], own_ref)
    forward(me, beside, own_ref)
    forward(me, above, own_ref)
    own_copy = pltpu.make_async_copy(own_ref, out_ref.at[me], own_sem)
    own_copy.start()

    def corner(k):
        shift = along[k] - me
        if k % 2 == 0:
            arrived(above + shift)
            forward(above + shift, beside)
        else:
            arrived(beside + shift)
            forward(beside + shift, above)

    for k in range(1, planes):
        arrived(along[k])
        forward(along[k], beside)
        forward(along[k], above)
        corner(k - 1)
    corner(planes - 1)
    across = beside + above - me
    for k in range(planes):
        shift = along[k] - me
        arrived((beside if k % 2 == 0 else above) + shift)
        arrived(across + shift)
    own_copy.wait()
    for copy in sent:
        copy.wait_send()


def gather_tokens(own):
    count = lax.axis_size("req")
    return pl.pallas_call(
        gather_kernel,
        out_shape=jax.ShapeDtypeStruct((count, *own.shape), own.dtype),
        in_specs=[pl.BlockSpec(memory_space=pltpu.VMEM)],
        out_specs=pl.BlockSpec(memory_space=pl.ANY),
        scratch_shapes=[
            pltpu.SemaphoreType.DMA((count,)),
            pltpu.SemaphoreType.DMA((count,)),
            pltpu.SemaphoreType.DMA,
        ],
        compiler_params=pltpu.CompilerParams(collective_id=0, has_side_effects=True),
    )(own)


def scatter_kernel(
    part_ref, out_ref, corner_in, beside_in, above_in, along_in, stage, send_sem, recv_sem
):
    me, beside, above, along = neighbours()
    planes = len(along)
    greet([beside, above] + along[1:])
    across = beside + above - me
    shifts = [along[k] - me for k in range(planes)]
    order = list(range(1, planes)) + [0]
    sent = []

    def send(source, target, slot, peer):
        copy = push(source, target, send_sem.at[len(sent)], recv_sem.at[slot], peer)
        sent.append(copy)

    def arrived(target, slot):
        pltpu.make_async_copy(target, target, recv_sem.at[slot]).wait()

    def wide(ref):
        return ref[...].astype(jnp.float32)

    for k in order:
        send(
            part_ref.at[across + shifts[k]], corner_in.at[k], k, beside if k % 2 == 0 else above
        )
    for k in order:
        if k % 2 == 0:
            send(part_ref.at[beside + shifts[k]], beside_in.at[k], planes + k, beside)
        else:
            send(part_ref.at[above + shifts[k]], above_in.at[k], 2 * planes + k, above)
    for k in order:
        arrived(corner_in.at[k], k)
        if k % 2 == 0:
            stage[k] = (wide(part_ref.at[above + shifts[k]]) + wide(corner_in.at[k])).astype(
                stage.dtype
            )
            send(stage.at[k], above_in.at[k], 2 * planes + k, above)
        else:
            stage[k] = (wide(part_ref.at[beside + shifts[k]]) + wide(corner_in.at[k])).astype(
                stage.dtype
            )
            send(stage.at[k], beside_in.at[k], planes + k, beside)
    for k in order:
        arrived(beside_in.at[k], planes + k)
        arrived(above_in.at[k], 2 * planes + k)
        total = wide(part_ref.at[along[k]]) + wide(beside_in.at[k]) + wide(above_in.at[k])
        if k:
            stage[planes + k] = total.astype(stage.dtype)
            send(stage.at[planes + k], along_in.at[k], 3 * planes + k, along[k])
        else:
            out_ref[...] = total
    for k in range(1, planes):
        arrived(along_in.at[k], 3 * planes + k)
        out_ref[...] += wide(along_in.at[k])
    for copy in sent:
        copy.wait_send()


def scatter_sums(part):
    count, rows, width = part.shape
    planes = count // 4
    block = (planes, rows, width)
    return pl.pallas_call(
        scatter_kernel,
        out_shape=jax.ShapeDtypeStruct((rows, width), jnp.float32),
        in_specs=[pl.BlockSpec(memory_space=pltpu.VMEM)],
        out_specs=pl.BlockSpec(memory_space=pltpu.VMEM),
        scratch_shapes=[
            pltpu.VMEM(block, part.dtype),
            pltpu.VMEM(block, part.dtype),
            pltpu.VMEM(block, part.dtype),
            pltpu.VMEM(block, part.dtype),
            pltpu.VMEM((2 * planes, rows, width), part.dtype),
            pltpu.SemaphoreType.DMA((4 * planes,)),
            pltpu.SemaphoreType.DMA((4 * planes,)),
        ],
        compiler_params=pltpu.CompilerParams(
            collective_id=1, has_side_effects=True, vmem_limit_bytes=40 * 1024 * 1024
        ),
    )(part)


def body(
    queries,
    cached_key_slots,
    cached_value_slots,
    new_token_keys,
    new_token_values,
    cache_len,
    placing,
    w_gate,
    w_up,
    w_down,
):
    slot_index = lax.axis_index("req")
    mlp_index = lax.axis_index("mlp")
    mlp_count = lax.axis_size("mlp")
    token_inputs = queries.shape[1]
    request_cache = cached_key_slots.shape[1]
    request_new_tokens = new_token_keys.shape[1]
    query_group_width = QUERY_HEADS // KEY_VALUE_HEADS
    row_count = token_inputs // mlp_count
    request = lookup(placing, slot_index)
    live_len = lookup(cache_len, request)
    query_head_rows = queries[0].reshape(
        token_inputs, KEY_VALUE_HEADS, query_group_width, HEAD_SIZE
    )
    request_keys = cached_key_slots[0].reshape(request_cache, KEY_VALUE_HEADS, HEAD_SIZE)
    request_values = cached_value_slots[0].reshape(request_cache, KEY_VALUE_HEADS, HEAD_SIZE)
    new_key_rows = new_token_keys[0].reshape(request_new_tokens, KEY_VALUE_HEADS, HEAD_SIZE)
    new_value_rows = new_token_values[0].reshape(request_new_tokens, KEY_VALUE_HEADS, HEAD_SIZE)
    cache_pos = mlp_index * request_cache + jnp.arange(request_cache, dtype=jnp.int32)
    cache_live = cache_pos < live_len
    scores_old = (
        jnp.einsum(
            "ngrd,cgd->grnc", query_head_rows, request_keys, preferred_element_type=jnp.float32
        )
        * score_scale
    )
    scores_old = jnp.where(cache_live[None, None, None, :], scores_old, negative)
    fresh_pos = mlp_index * request_new_tokens + jnp.arange(request_new_tokens, dtype=jnp.int32)
    causal = fresh_pos[None, :] <= jnp.arange(token_inputs, dtype=jnp.int32)[:, None]
    scores_new = (
        jnp.einsum(
            "ngrd,mgd->grnm", query_head_rows, new_key_rows, preferred_element_type=jnp.float32
        )
        * score_scale
    )
    scores_new = jnp.where(causal[None, None], scores_new, negative)
    local_top = jnp.maximum(scores_old.max(-1), scores_new.max(-1))
    row_top = lax.pmax(local_top, "mlp")
    expo_old = jnp.exp(scores_old - row_top[..., None])
    expo_new = jnp.exp(scores_new - row_top[..., None])
    denom_local = expo_old.sum(-1) + expo_new.sum(-1)
    probs_old = expo_old.astype(jnp.bfloat16)
    probs_new = expo_new.astype(jnp.bfloat16)
    weighted = jnp.einsum(
        "grnc,cgd->ngrd", probs_old, request_values, preferred_element_type=jnp.float32
    )
    weighted = weighted + jnp.einsum(
        "grnm,mgd->ngrd", probs_new, new_value_rows, preferred_element_type=jnp.float32
    )
    if lax.axis_size("req") != 16:
        return gathered_weights(weighted, denom_local, w_gate, w_up, w_down)
    weights = jnp.stack([w_gate, w_up, w_down.T])
    weights = lax.all_to_all(weights, "req", split_axis=2, concat_axis=1, tiled=True)
    weights = lax.all_gather(weights, "mlp", axis=2, tiled=True)
    denom_rows = jnp.transpose(denom_local, (2, 0, 1))
    weighted = lax.psum_scatter(weighted, "mlp", scatter_dimension=0, tiled=True)
    denom = lax.psum_scatter(denom_rows, "mlp", scatter_dimension=0, tiled=True)
    attended = (
        (weighted / denom[..., None])
        .reshape(row_count, QUERY_HEADS * HEAD_SIZE)
        .astype(jnp.bfloat16)
    )
    normed = gather_tokens(rms_rows(attended)).reshape(-1, attended.shape[1])
    gate_sum = jnp.dot(normed, weights[0], preferred_element_type=jnp.float32)
    upper_sum = jnp.dot(normed, weights[1], preferred_element_type=jnp.float32)
    hidden = (jax.nn.silu(gate_sum) * upper_sum).astype(jnp.bfloat16)
    partial_down = lax.dot_general(
        hidden, weights[2], (((1,), (1,)), ((), ())), preferred_element_type=jnp.float32
    )
    own_rows = scatter_sums(partial_down.astype(jnp.bfloat16).reshape(-1, *attended.shape))
    return (attended.astype(jnp.float32) + own_rows).astype(jnp.bfloat16)[None]


def solution(mesh):
    in_specs = (
        P("req", None, None),
        P("req", "mlp", None),
        P("req", "mlp", None),
        P("req", "mlp", None),
        P("req", "mlp", None),
        P(),
        P(),
        P("req", "mlp"),
        P("req", "mlp"),
        P("mlp", "req"),
    )
    out_specs = P("req", "mlp", None)
    return jax.shard_map(body, mesh=mesh, in_specs=in_specs, out_specs=out_specs, check_vma=False)
```

```python
import jax
import jax.numpy as jnp
from jax import lax
from jax.experimental import pallas as pl
from jax.experimental.pallas import tpu as pltpu
from jax.sharding import PartitionSpec as P

HEAD_SIZE = 256
QUERY_HEADS = 6
KEY_VALUE_HEADS = 2


score_scale = 0.0625
negative = -1e30


def lookup(table, index):
    positions = jnp.arange(table.shape[0], dtype=jnp.int32)
    return jnp.sum(jnp.where(positions == index, table, 0))


def rms_rows(attended):
    wide = attended.astype(jnp.float32)
    return (wide * lax.rsqrt(jnp.mean(wide * wide, axis=-1, keepdims=True) + 1e-06)).astype(
        jnp.bfloat16
    )


def wide_body(
    queries,
    cached_key_slots,
    cached_value_slots,
    new_token_keys,
    new_token_values,
    cache_len,
    placing,
    w_gate,
    w_up,
    w_down,
):
    slot_index = lax.axis_index("req")
    mlp_index = lax.axis_index("mlp")
    mlp_count = lax.axis_size("mlp")
    token_inputs = queries.shape[1]
    request_cache = cached_key_slots.shape[1]
    request_new_tokens = new_token_keys.shape[1]
    query_group_width = QUERY_HEADS // KEY_VALUE_HEADS
    row_count = token_inputs // mlp_count
    request = lookup(placing, slot_index)
    live_len = lookup(cache_len, request)
    query_head_rows = queries[0].reshape(
        token_inputs, KEY_VALUE_HEADS, query_group_width, HEAD_SIZE
    )
    request_keys = cached_key_slots[0].reshape(request_cache, KEY_VALUE_HEADS, HEAD_SIZE)
    request_values = cached_value_slots[0].reshape(request_cache, KEY_VALUE_HEADS, HEAD_SIZE)
    new_key_rows = new_token_keys[0].reshape(request_new_tokens, KEY_VALUE_HEADS, HEAD_SIZE)
    new_value_rows = new_token_values[0].reshape(request_new_tokens, KEY_VALUE_HEADS, HEAD_SIZE)
    cache_pos = mlp_index * request_cache + jnp.arange(request_cache, dtype=jnp.int32)
    cache_live = cache_pos < live_len
    scores_old = (
        jnp.einsum(
            "ngrd,cgd->grnc", query_head_rows, request_keys, preferred_element_type=jnp.float32
        )
        * score_scale
    )
    scores_old = jnp.where(cache_live[None, None, None, :], scores_old, negative)
    fresh_pos = mlp_index * request_new_tokens + jnp.arange(request_new_tokens, dtype=jnp.int32)
    causal = fresh_pos[None, :] <= jnp.arange(token_inputs, dtype=jnp.int32)[:, None]
    scores_new = (
        jnp.einsum(
            "ngrd,mgd->grnm", query_head_rows, new_key_rows, preferred_element_type=jnp.float32
        )
        * score_scale
    )
    scores_new = jnp.where(causal[None, None], scores_new, negative)
    local_top = jnp.maximum(scores_old.max(-1), scores_new.max(-1))
    row_top = lax.pmax(local_top, "mlp")
    expo_old = jnp.exp(scores_old - row_top[..., None])
    expo_new = jnp.exp(scores_new - row_top[..., None])
    denom_local = expo_old.sum(-1) + expo_new.sum(-1)
    probs_old = expo_old.astype(jnp.bfloat16)
    probs_new = expo_new.astype(jnp.bfloat16)
    weighted = jnp.einsum(
        "grnc,cgd->ngrd", probs_old, request_values, preferred_element_type=jnp.float32
    )
    weighted = weighted + jnp.einsum(
        "grnm,mgd->ngrd", probs_new, new_value_rows, preferred_element_type=jnp.float32
    )
    weighted, denom = lax.psum((weighted, denom_local), "mlp")
    attended = (
        (weighted / jnp.transpose(denom, (2, 0, 1))[..., None])
        .reshape(token_inputs, QUERY_HEADS * HEAD_SIZE)
        .astype(jnp.bfloat16)
    )
    normed = rms_rows(attended)
    own_attended = lax.dynamic_slice_in_dim(attended, mlp_index * row_count, row_count, 0)
    gate_sum = jnp.dot(
        normed,
        lax.all_gather(w_gate, "req", axis=0, tiled=True),
        preferred_element_type=jnp.float32,
    )
    upper_sum = jnp.dot(
        normed, lax.all_gather(w_up, "req", axis=0, tiled=True), preferred_element_type=jnp.float32
    )
    hidden = (jax.nn.silu(gate_sum) * upper_sum).astype(jnp.bfloat16)
    partial_down = jnp.dot(
        hidden,
        lax.all_gather(w_down, "req", axis=1, tiled=True),
        preferred_element_type=jnp.float32,
    )
    own_rows = lax.psum_scatter(
        partial_down.astype(jnp.bfloat16), "mlp", scatter_dimension=0, tiled=True
    ).astype(jnp.float32)
    residual = own_attended.astype(jnp.float32)
    return (residual + own_rows).astype(jnp.bfloat16)[None]


def neighbours():
    me = lax.axis_index("req")
    planes = lax.axis_size("req") // 4
    plane, place = me // 4, me % 4
    beside = plane * 4 + place + 1 - 2 * (place % 2)
    above = plane * 4 + (place + 2) % 4
    along = [((plane + k) % planes) * 4 + place for k in range(planes)]
    return me, beside, above, along


def greet(peers):
    barrier = pltpu.get_barrier_semaphore()
    for peer in peers:
        pl.semaphore_signal(
            barrier, inc=1, device_id={"req": peer}, device_id_type=pl.DeviceIdType.MESH
        )
    pl.semaphore_wait(barrier, len(peers))


def push(source, target, send_sem, recv_sem, peer):
    copy = pltpu.make_async_remote_copy(
        src_ref=source,
        dst_ref=target,
        send_sem=send_sem,
        recv_sem=recv_sem,
        device_id={"req": peer},
        device_id_type=pl.DeviceIdType.MESH,
    )
    copy.start()
    return copy


def gather_kernel(own_ref, out_ref, send_sem, recv_sem, own_sem):
    me, beside, above, along = neighbours()
    planes = len(along)
    greet([beside, above] + along[1:])
    sent = []

    def forward(block, peer, source=None):
        sent.append(
            push(
                out_ref.at[block] if source is None else source,
                out_ref.at[block],
                send_sem.at[len(sent)],
                recv_sem.at[block],
                peer,
            )
        )

    def arrived(block):
        pltpu.make_async_copy(out_ref.at[block], out_ref.at[block], recv_sem.at[block]).wait()

    for k in range(1, planes):
        forward(me, along[k], own_ref)
    forward(me, beside, own_ref)
    forward(me, above, own_ref)
    own_copy = pltpu.make_async_copy(own_ref, out_ref.at[me], own_sem)
    own_copy.start()

    def corner(k):
        shift = along[k] - me
        if k % 2 == 0:
            arrived(above + shift)
            forward(above + shift, beside)
        else:
            arrived(beside + shift)
            forward(beside + shift, above)

    for k in range(1, planes):
        arrived(along[k])
        forward(along[k], beside)
        forward(along[k], above)
        corner(k - 1)
    corner(planes - 1)
    across = beside + above - me
    for k in range(planes):
        shift = along[k] - me
        arrived((beside if k % 2 == 0 else above) + shift)
        arrived(across + shift)
    own_copy.wait()
    for copy in sent:
        copy.wait_send()


def gather_tokens(own):
    count = lax.axis_size("req")
    return pl.pallas_call(
        gather_kernel,
        out_shape=jax.ShapeDtypeStruct((count, *own.shape), own.dtype),
        in_specs=[pl.BlockSpec(memory_space=pltpu.VMEM)],
        out_specs=pl.BlockSpec(memory_space=pl.ANY),
        scratch_shapes=[
            pltpu.SemaphoreType.DMA((count,)),
            pltpu.SemaphoreType.DMA((count,)),
            pltpu.SemaphoreType.DMA,
        ],
        compiler_params=pltpu.CompilerParams(collective_id=0, has_side_effects=True),
    )(own)


def scatter_kernel(
    part_ref, out_ref, corner_in, beside_in, above_in, along_in, stage, send_sem, recv_sem
):
    me, beside, above, along = neighbours()
    planes = len(along)
    greet([beside, above] + along[1:])
    across = beside + above - me
    shifts = [along[k] - me for k in range(planes)]
    order = list(range(1, planes)) + [0]
    sent = []

    def send(source, target, slot, peer):
        copy = push(source, target, send_sem.at[len(sent)], recv_sem.at[slot], peer)
        sent.append(copy)

    def arrived(target, slot):
        pltpu.make_async_copy(target, target, recv_sem.at[slot]).wait()

    def wide(ref):
        return ref[...].astype(jnp.float32)

    for k in order:
        send(
            part_ref.at[across + shifts[k]], corner_in.at[k], k, beside if k % 2 == 0 else above
        )
    for k in order:
        if k % 2 == 0:
            send(part_ref.at[beside + shifts[k]], beside_in.at[k], planes + k, beside)
        else:
            send(part_ref.at[above + shifts[k]], above_in.at[k], 2 * planes + k, above)
    for k in order:
        arrived(corner_in.at[k], k)
        if k % 2 == 0:
            stage[k] = (wide(part_ref.at[above + shifts[k]]) + wide(corner_in.at[k])).astype(
                stage.dtype
            )
            send(stage.at[k], above_in.at[k], 2 * planes + k, above)
        else:
            stage[k] = (wide(part_ref.at[beside + shifts[k]]) + wide(corner_in.at[k])).astype(
                stage.dtype
            )
            send(stage.at[k], beside_in.at[k], planes + k, beside)
    for k in order:
        arrived(beside_in.at[k], planes + k)
        arrived(above_in.at[k], 2 * planes + k)
        total = wide(part_ref.at[along[k]]) + wide(beside_in.at[k]) + wide(above_in.at[k])
        if k:
            stage[planes + k] = total.astype(stage.dtype)
            send(stage.at[planes + k], along_in.at[k], 3 * planes + k, along[k])
        else:
            out_ref[...] = total
    for k in range(1, planes):
        arrived(along_in.at[k], 3 * planes + k)
        out_ref[...] += wide(along_in.at[k])
    for copy in sent:
        copy.wait_send()


def scatter_sums(part):
    count, rows, width = part.shape
    planes = count // 4
    block = (planes, rows, width)
    return pl.pallas_call(
        scatter_kernel,
        out_shape=jax.ShapeDtypeStruct((rows, width), jnp.float32),
        in_specs=[pl.BlockSpec(memory_space=pltpu.VMEM)],
        out_specs=pl.BlockSpec(memory_space=pltpu.VMEM),
        scratch_shapes=[
            pltpu.VMEM(block, part.dtype),
            pltpu.VMEM(block, part.dtype),
            pltpu.VMEM(block, part.dtype),
            pltpu.VMEM(block, part.dtype),
            pltpu.VMEM((2 * planes, rows, width), part.dtype),
            pltpu.SemaphoreType.DMA((4 * planes,)),
            pltpu.SemaphoreType.DMA((4 * planes,)),
        ],
        compiler_params=pltpu.CompilerParams(
            collective_id=1, has_side_effects=True, vmem_limit_bytes=40 * 1024 * 1024
        ),
    )(part)


def attend_half(queries, keys, values, new_keys, new_values, cache_live, causal):
    scores_old = jnp.dot(queries, keys.T, preferred_element_type=jnp.float32) * score_scale
    scores_old = jnp.where(cache_live[None, :], scores_old, negative)
    scores_new = jnp.dot(queries, new_keys.T, preferred_element_type=jnp.float32) * score_scale
    scores_new = jnp.where(causal, scores_new, negative)
    top = jnp.maximum(scores_old.max(-1), scores_new.max(-1))
    expo_old = jnp.exp(scores_old - top[:, None])
    expo_new = jnp.exp(scores_new - top[:, None])
    denom = expo_old.sum(-1) + expo_new.sum(-1)
    weighted = jnp.dot(expo_old.astype(jnp.bfloat16), values, preferred_element_type=jnp.float32)
    weighted = weighted + jnp.dot(
        expo_new.astype(jnp.bfloat16), new_values, preferred_element_type=jnp.float32
    )
    return top, denom, weighted


def feed_forward(normed, weights):
    gate_sum = jnp.dot(normed, weights[0], preferred_element_type=jnp.float32)
    upper_sum = jnp.dot(normed, weights[1], preferred_element_type=jnp.float32)
    hidden = (jax.nn.silu(gate_sum) * upper_sum).astype(jnp.bfloat16)
    return lax.dot_general(
        hidden, weights[2], (((1,), (1,)), ((), ())), preferred_element_type=jnp.float32
    )


def body(
    queries,
    cached_key_slots,
    cached_value_slots,
    new_token_keys,
    new_token_values,
    cache_len,
    placing,
    w_gate,
    w_up,
    w_down,
):
    count = lax.axis_size("req")
    if count != 16 or lax.axis_size("mlp") != 2:
        return wide_body(
            queries,
            cached_key_slots,
            cached_value_slots,
            new_token_keys,
            new_token_values,
            cache_len,
            placing,
            w_gate,
            w_up,
            w_down,
        )
    mlp_index = lax.axis_index("mlp")
    swap = [(0, 1), (1, 0)]
    packed = jnp.stack(
        [w.reshape(w.shape[0], count, -1).transpose(1, 0, 2) for w in (w_gate, w_up, w_down.T)],
        axis=1,
    )
    landed = lax.all_to_all(packed, "req", split_axis=0, concat_axis=0, tiled=True)

    live_len = lookup(cache_len, lookup(placing, lax.axis_index("req")))
    tokens, width = queries.shape[1:]
    request_cache, request_new = cached_key_slots.shape[1], new_token_keys.shape[1]
    group = QUERY_HEADS // KEY_VALUE_HEADS
    cache_pos = mlp_index * request_cache + jnp.arange(request_cache, dtype=jnp.int32)
    fresh_pos = mlp_index * request_new + jnp.arange(request_new, dtype=jnp.int32)
    token_pos = jnp.tile(jnp.arange(tokens, dtype=jnp.int32), group)
    causal = fresh_pos[None, :] <= token_pos[:, None]
    found = []
    for g in range(KEY_VALUE_HEADS):
        head = slice(g * HEAD_SIZE, (g + 1) * HEAD_SIZE)
        heads = range(g * group, (g + 1) * group)
        found.append(
            attend_half(
                jnp.concatenate(
                    [queries[0, :, h * HEAD_SIZE : (h + 1) * HEAD_SIZE] for h in heads], axis=0
                ),
                cached_key_slots[0, :, head],
                cached_value_slots[0, :, head],
                new_token_keys[0, :, head],
                new_token_values[0, :, head],
                cache_pos < live_len,
                causal,
            )
        )
    top, denom, weighted = (
        jnp.stack(parts).reshape(QUERY_HEADS, tokens, -1) for parts in zip(*found)
    )
    rows = tokens // 2

    def halves(x):
        own = lax.dynamic_slice_in_dim(x, mlp_index * rows, rows, 1)
        away = lax.dynamic_slice_in_dim(x, (1 - mlp_index) * rows, rows, 1)
        return own, lax.ppermute(away, "mlp", swap)

    own_stats, peer_stats = halves(jnp.concatenate([top, denom], axis=2))
    own_weighted, peer_weighted = halves(weighted)
    row_top = jnp.maximum(own_stats[..., :1], peer_stats[..., :1])
    own_scale = jnp.exp(own_stats[..., :1] - row_top)
    peer_scale = jnp.exp(peer_stats[..., :1] - row_top)
    attended = (own_weighted * own_scale + peer_weighted * peer_scale) / (
        own_stats[..., 1:] * own_scale + peer_stats[..., 1:] * peer_scale
    )
    attended = attended.transpose(1, 0, 2).reshape(rows, width).astype(jnp.bfloat16)
    normed = gather_tokens(rms_rows(attended)).reshape(-1, width)
    landed, normed = lax.optimization_barrier((landed, normed))
    weights = landed.transpose(1, 0, 2, 3).reshape(3, width, -1)
    peer_weights = lax.ppermute(weights, "mlp", swap)
    partial_down = feed_forward(normed, weights) + feed_forward(normed, peer_weights)
    own_rows = scatter_sums(partial_down.astype(jnp.bfloat16).reshape(count, rows, width))
    return (attended.astype(jnp.float32) + own_rows).astype(jnp.bfloat16)[None]


def solution(mesh):
    in_specs = (
        P("req", None, None),
        P("req", "mlp", None),
        P("req", "mlp", None),
        P("req", "mlp", None),
        P("req", "mlp", None),
        P(),
        P(),
        P("req", "mlp"),
        P("req", "mlp"),
        P("mlp", "req"),
    )
    out_specs = P("req", "mlp", None)
    return jax.shard_map(body, mesh=mesh, in_specs=in_specs, out_specs=out_specs, check_vma=False)
```

```python
import jax
import jax.numpy as jnp
from jax import lax
from jax.experimental import pallas as pl
from jax.experimental.pallas import tpu as pltpu
from jax.sharding import PartitionSpec as P

HEAD_SIZE = 256
QUERY_HEADS = 6
KEY_VALUE_HEADS = 2


score_scale = 0.0625
negative = -1e30


def lookup(table, index):
    positions = jnp.arange(table.shape[0], dtype=jnp.int32)
    return jnp.sum(jnp.where(positions == index, table, 0))


def rms_rows(attended):
    wide = attended.astype(jnp.float32)
    return (wide * lax.rsqrt(jnp.mean(wide * wide, axis=-1, keepdims=True) + 1e-06)).astype(
        jnp.bfloat16
    )


def wide_body(
    queries,
    cached_key_slots,
    cached_value_slots,
    new_token_keys,
    new_token_values,
    cache_len,
    placing,
    w_gate,
    w_up,
    w_down,
):
    slot_index = lax.axis_index("req")
    mlp_index = lax.axis_index("mlp")
    mlp_count = lax.axis_size("mlp")
    token_inputs = queries.shape[1]
    request_cache = cached_key_slots.shape[1]
    request_new_tokens = new_token_keys.shape[1]
    query_group_width = QUERY_HEADS // KEY_VALUE_HEADS
    row_count = token_inputs // mlp_count
    request = lookup(placing, slot_index)
    live_len = lookup(cache_len, request)
    query_head_rows = queries[0].reshape(
        token_inputs, KEY_VALUE_HEADS, query_group_width, HEAD_SIZE
    )
    request_keys = cached_key_slots[0].reshape(request_cache, KEY_VALUE_HEADS, HEAD_SIZE)
    request_values = cached_value_slots[0].reshape(request_cache, KEY_VALUE_HEADS, HEAD_SIZE)
    new_key_rows = new_token_keys[0].reshape(request_new_tokens, KEY_VALUE_HEADS, HEAD_SIZE)
    new_value_rows = new_token_values[0].reshape(request_new_tokens, KEY_VALUE_HEADS, HEAD_SIZE)
    cache_pos = mlp_index * request_cache + jnp.arange(request_cache, dtype=jnp.int32)
    cache_live = cache_pos < live_len
    scores_old = (
        jnp.einsum(
            "ngrd,cgd->grnc", query_head_rows, request_keys, preferred_element_type=jnp.float32
        )
        * score_scale
    )
    scores_old = jnp.where(cache_live[None, None, None, :], scores_old, negative)
    fresh_pos = mlp_index * request_new_tokens + jnp.arange(request_new_tokens, dtype=jnp.int32)
    causal = fresh_pos[None, :] <= jnp.arange(token_inputs, dtype=jnp.int32)[:, None]
    scores_new = (
        jnp.einsum(
            "ngrd,mgd->grnm", query_head_rows, new_key_rows, preferred_element_type=jnp.float32
        )
        * score_scale
    )
    scores_new = jnp.where(causal[None, None], scores_new, negative)
    local_top = jnp.maximum(scores_old.max(-1), scores_new.max(-1))
    row_top = lax.pmax(local_top, "mlp")
    expo_old = jnp.exp(scores_old - row_top[..., None])
    expo_new = jnp.exp(scores_new - row_top[..., None])
    denom_local = expo_old.sum(-1) + expo_new.sum(-1)
    probs_old = expo_old.astype(jnp.bfloat16)
    probs_new = expo_new.astype(jnp.bfloat16)
    weighted = jnp.einsum(
        "grnc,cgd->ngrd", probs_old, request_values, preferred_element_type=jnp.float32
    )
    weighted = weighted + jnp.einsum(
        "grnm,mgd->ngrd", probs_new, new_value_rows, preferred_element_type=jnp.float32
    )
    weighted, denom = lax.psum((weighted, denom_local), "mlp")
    attended = (
        (weighted / jnp.transpose(denom, (2, 0, 1))[..., None])
        .reshape(token_inputs, QUERY_HEADS * HEAD_SIZE)
        .astype(jnp.bfloat16)
    )
    normed = rms_rows(attended)
    own_attended = lax.dynamic_slice_in_dim(attended, mlp_index * row_count, row_count, 0)
    gate_sum = jnp.dot(
        normed,
        lax.all_gather(w_gate, "req", axis=0, tiled=True),
        preferred_element_type=jnp.float32,
    )
    upper_sum = jnp.dot(
        normed, lax.all_gather(w_up, "req", axis=0, tiled=True), preferred_element_type=jnp.float32
    )
    hidden = (jax.nn.silu(gate_sum) * upper_sum).astype(jnp.bfloat16)
    partial_down = jnp.dot(
        hidden,
        lax.all_gather(w_down, "req", axis=1, tiled=True),
        preferred_element_type=jnp.float32,
    )
    own_rows = lax.psum_scatter(
        partial_down.astype(jnp.bfloat16), "mlp", scatter_dimension=0, tiled=True
    ).astype(jnp.float32)
    residual = own_attended.astype(jnp.float32)
    return (residual + own_rows).astype(jnp.bfloat16)[None]


def neighbours():
    me = lax.axis_index("req")
    planes = lax.axis_size("req") // 4
    plane, place = me // 4, me % 4
    beside = plane * 4 + place + 1 - 2 * (place % 2)
    above = plane * 4 + (place + 2) % 4
    along = [((plane + k) % planes) * 4 + place for k in range(planes)]
    return me, beside, above, along


def greet(peers):
    barrier = pltpu.get_barrier_semaphore()
    for peer in peers:
        pl.semaphore_signal(
            barrier, inc=1, device_id={"req": peer}, device_id_type=pl.DeviceIdType.MESH
        )
    pl.semaphore_wait(barrier, len(peers))


def push(source, target, send_sem, recv_sem, peer):
    copy = pltpu.make_async_remote_copy(
        src_ref=source,
        dst_ref=target,
        send_sem=send_sem,
        recv_sem=recv_sem,
        device_id={"req": peer},
        device_id_type=pl.DeviceIdType.MESH,
    )
    copy.start()
    return copy


def gather_kernel(own_ref, out_ref, send_sem, recv_sem, own_sem):
    me, beside, above, along = neighbours()
    planes = len(along)
    greet([beside, above] + along[1:])
    sent = []

    def forward(block, peer, source=None):
        sent.append(
            push(
                out_ref.at[block] if source is None else source,
                out_ref.at[block],
                send_sem.at[len(sent)],
                recv_sem.at[block],
                peer,
            )
        )

    def arrived(block):
        pltpu.make_async_copy(out_ref.at[block], out_ref.at[block], recv_sem.at[block]).wait()

    for k in range(1, planes):
        forward(me, along[k], own_ref)
    forward(me, beside, own_ref)
    forward(me, above, own_ref)
    own_copy = pltpu.make_async_copy(own_ref, out_ref.at[me], own_sem)
    own_copy.start()

    def corner(k):
        shift = along[k] - me
        if k % 2 == 0:
            arrived(above + shift)
            forward(above + shift, beside)
        else:
            arrived(beside + shift)
            forward(beside + shift, above)

    for k in range(1, planes):
        arrived(along[k])
        forward(along[k], beside)
        forward(along[k], above)
        corner(k - 1)
    corner(planes - 1)
    across = beside + above - me
    for k in range(planes):
        shift = along[k] - me
        arrived((beside if k % 2 == 0 else above) + shift)
        arrived(across + shift)
    own_copy.wait()
    for copy in sent:
        copy.wait_send()


def gather_tokens(own):
    count = lax.axis_size("req")
    return pl.pallas_call(
        gather_kernel,
        out_shape=jax.ShapeDtypeStruct((count, *own.shape), own.dtype),
        in_specs=[pl.BlockSpec(memory_space=pltpu.VMEM)],
        out_specs=pl.BlockSpec(memory_space=pl.ANY),
        scratch_shapes=[
            pltpu.SemaphoreType.DMA((count,)),
            pltpu.SemaphoreType.DMA((count,)),
            pltpu.SemaphoreType.DMA,
        ],
        compiler_params=pltpu.CompilerParams(collective_id=0, has_side_effects=True),
    )(own)


def scatter_kernel(
    part_ref, out_ref, corner_in, beside_in, above_in, along_in, stage, send_sem, recv_sem
):
    me, beside, above, along = neighbours()
    planes = len(along)
    greet([beside, above] + along[1:])
    across = beside + above - me
    shifts = [along[k] - me for k in range(planes)]
    order = list(range(1, planes)) + [0]
    sent = []

    def send(source, target, slot, peer):
        copy = push(source, target, send_sem.at[len(sent)], recv_sem.at[slot], peer)
        sent.append(copy)

    def arrived(target, slot):
        pltpu.make_async_copy(target, target, recv_sem.at[slot]).wait()

    def wide(ref):
        return ref[...].astype(jnp.float32)

    def corner(k):
        send(
            part_ref.at[across + shifts[k]], corner_in.at[k], k, beside if k % 2 == 0 else above
        )

    def direct(k):
        if k % 2 == 0:
            send(part_ref.at[beside + shifts[k]], beside_in.at[k], planes + k, beside)
        else:
            send(part_ref.at[above + shifts[k]], above_in.at[k], 2 * planes + k, above)

    def staged(k):
        arrived(corner_in.at[k], k)
        if k % 2 == 0:
            stage[k] = (wide(part_ref.at[above + shifts[k]]) + wide(corner_in.at[k])).astype(
                stage.dtype
            )
            send(stage.at[k], above_in.at[k], 2 * planes + k, above)
        else:
            stage[k] = (wide(part_ref.at[beside + shifts[k]]) + wide(corner_in.at[k])).astype(
                stage.dtype
            )
            send(stage.at[k], beside_in.at[k], planes + k, beside)

    def finish(k):
        arrived(beside_in.at[k], planes + k)
        arrived(above_in.at[k], 2 * planes + k)
        total = wide(part_ref.at[along[k]]) + wide(beside_in.at[k]) + wide(above_in.at[k])
        if k:
            stage[planes + k] = total.astype(stage.dtype)
            send(stage.at[planes + k], along_in.at[k], 3 * planes + k, along[k])
        else:
            out_ref[...] = total

    for start in range(0, planes, 2):
        pair = order[start : start + 2]
        for step in (corner, direct):
            for k in pair:
                step(k)
        if start:
            for k in order[start - 2 : start]:
                finish(k)
        for k in pair:
            staged(k)
    for k in order[planes - 2 :]:
        finish(k)
    for k in range(1, planes):
        arrived(along_in.at[k], 3 * planes + k)
        out_ref[...] += wide(along_in.at[k])
    for copy in sent:
        copy.wait_send()


def scatter_sums(part):
    count, rows, width = part.shape
    planes = count // 4
    block = (planes, rows, width)
    return pl.pallas_call(
        scatter_kernel,
        out_shape=jax.ShapeDtypeStruct((rows, width), jnp.float32),
        in_specs=[pl.BlockSpec(memory_space=pltpu.VMEM)],
        out_specs=pl.BlockSpec(memory_space=pltpu.VMEM),
        scratch_shapes=[
            pltpu.VMEM(block, part.dtype),
            pltpu.VMEM(block, part.dtype),
            pltpu.VMEM(block, part.dtype),
            pltpu.VMEM(block, part.dtype),
            pltpu.VMEM((2 * planes, rows, width), part.dtype),
            pltpu.SemaphoreType.DMA((4 * planes,)),
            pltpu.SemaphoreType.DMA((4 * planes,)),
        ],
        compiler_params=pltpu.CompilerParams(
            collective_id=1, has_side_effects=True, vmem_limit_bytes=40 * 1024 * 1024
        ),
    )(part)


def attend_half(queries, keys, values, new_keys, new_values, cache_live, causal):
    scores_old = jnp.dot(queries, keys.T, preferred_element_type=jnp.float32) * score_scale
    scores_old = jnp.where(cache_live[None, :], scores_old, negative)
    scores_new = jnp.dot(queries, new_keys.T, preferred_element_type=jnp.float32) * score_scale
    scores_new = jnp.where(causal, scores_new, negative)
    top = jnp.maximum(scores_old.max(-1), scores_new.max(-1))
    expo_old = jnp.exp(scores_old - top[:, None])
    expo_new = jnp.exp(scores_new - top[:, None])
    denom = expo_old.sum(-1) + expo_new.sum(-1)
    weighted = jnp.dot(expo_old.astype(jnp.bfloat16), values, preferred_element_type=jnp.float32)
    weighted = weighted + jnp.dot(
        expo_new.astype(jnp.bfloat16), new_values, preferred_element_type=jnp.float32
    )
    return top, denom, weighted


def hidden_units(normed, weights):
    gate_sum = jnp.dot(normed, weights[0], preferred_element_type=jnp.float32)
    upper_sum = jnp.dot(normed, weights[1], preferred_element_type=jnp.float32)
    return (jax.nn.silu(gate_sum) * upper_sum).astype(jnp.bfloat16)


def body(
    queries,
    cached_key_slots,
    cached_value_slots,
    new_token_keys,
    new_token_values,
    cache_len,
    placing,
    w_gate,
    w_up,
    w_down,
):
    count = lax.axis_size("req")
    if count != 16 or lax.axis_size("mlp") != 2:
        return wide_body(
            queries,
            cached_key_slots,
            cached_value_slots,
            new_token_keys,
            new_token_values,
            cache_len,
            placing,
            w_gate,
            w_up,
            w_down,
        )
    mlp_index = lax.axis_index("mlp")
    swap = [(0, 1), (1, 0)]
    packed = jnp.stack(
        [w.reshape(w.shape[0], count, -1).transpose(1, 0, 2) for w in (w_gate, w_up, w_down.T)],
        axis=1,
    )
    landed = lax.all_to_all(packed, "req", split_axis=0, concat_axis=0, tiled=True)

    live_len = lookup(cache_len, lookup(placing, lax.axis_index("req")))
    tokens, width = queries.shape[1:]
    request_cache, request_new = cached_key_slots.shape[1], new_token_keys.shape[1]
    group = QUERY_HEADS // KEY_VALUE_HEADS
    cache_pos = mlp_index * request_cache + jnp.arange(request_cache, dtype=jnp.int32)
    fresh_pos = mlp_index * request_new + jnp.arange(request_new, dtype=jnp.int32)
    token_pos = jnp.tile(jnp.arange(tokens, dtype=jnp.int32), group)
    causal = fresh_pos[None, :] <= token_pos[:, None]
    found = []
    for g in range(KEY_VALUE_HEADS):
        head = slice(g * HEAD_SIZE, (g + 1) * HEAD_SIZE)
        heads = range(g * group, (g + 1) * group)
        found.append(
            attend_half(
                jnp.concatenate(
                    [queries[0, :, h * HEAD_SIZE : (h + 1) * HEAD_SIZE] for h in heads], axis=0
                ),
                cached_key_slots[0, :, head],
                cached_value_slots[0, :, head],
                new_token_keys[0, :, head],
                new_token_values[0, :, head],
                cache_pos < live_len,
                causal,
            )
        )
    top, denom, weighted = (
        jnp.stack(parts).reshape(QUERY_HEADS, tokens, -1) for parts in zip(*found)
    )
    rows = tokens // 2

    def halves(x):
        own = lax.dynamic_slice_in_dim(x, mlp_index * rows, rows, 1)
        away = lax.dynamic_slice_in_dim(x, (1 - mlp_index) * rows, rows, 1)
        return own, lax.ppermute(away, "mlp", swap)

    own_stats, peer_stats = halves(jnp.concatenate([top, denom], axis=2))
    own_weighted, peer_weighted = halves(weighted)
    row_top = jnp.maximum(own_stats[..., :1], peer_stats[..., :1])
    own_scale = jnp.exp(own_stats[..., :1] - row_top)
    peer_scale = jnp.exp(peer_stats[..., :1] - row_top)
    attended = (own_weighted * own_scale + peer_weighted * peer_scale) / (
        own_stats[..., 1:] * own_scale + peer_stats[..., 1:] * peer_scale
    )
    attended = attended.transpose(1, 0, 2).reshape(rows, width).astype(jnp.bfloat16)
    normed = gather_tokens(rms_rows(attended)).reshape(-1, width)
    landed, normed = lax.optimization_barrier((landed, normed))
    weights = landed.transpose(1, 0, 2, 3).reshape(3, width, -1)
    peer_weights = lax.ppermute(weights, "mlp", swap)
    hidden = jnp.concatenate(
        [hidden_units(normed, weights), hidden_units(normed, peer_weights)], axis=1
    )
    partial_down = lax.dot_general(
        hidden,
        jnp.concatenate([weights[2], peer_weights[2]], axis=1),
        (((1,), (1,)), ((), ())),
        preferred_element_type=jnp.float32,
    )
    own_rows = scatter_sums(partial_down.astype(jnp.bfloat16).reshape(count, rows, width))
    return (attended.astype(jnp.float32) + own_rows).astype(jnp.bfloat16)[None]


def solution(mesh):
    in_specs = (
        P("req", None, None),
        P("req", "mlp", None),
        P("req", "mlp", None),
        P("req", "mlp", None),
        P("req", "mlp", None),
        P(),
        P(),
        P("req", "mlp"),
        P("req", "mlp"),
        P("mlp", "req"),
    )
    out_specs = P("req", "mlp", None)
    return jax.shard_map(body, mesh=mesh, in_specs=in_specs, out_specs=out_specs, check_vma=False)
```
